32 devices in a mesh: rows: 8 (over z, y), scen: 4 (over x, core).
Axes of the slice: x: 2, y: 2, z: 4, core: 2. Of those that a mesh axis runs over, the one named last changes fastest.
Arguments:
- inverse: bfloat16 [4096, 16384], P('scen', 'rows'), as said below
- voltage_prev: float32 [64, 16384], P('scen', 'rows'), may hold values from -6 to 6
- line_delay: int32 [8, 16], P('rows'), may hold values from 0 to 4, as said below
- line_bus: int32 [8, 16], P('rows'), may hold values from 0 to 2047
- line_impedance: float32 [8, 16], P('rows'), may hold values from 0.5 to 2, as said below
- line_past: float32 [4, 2, 64, 8, 16], P(None, None, 'scen', 'rows'), may hold values from -6 to 6
- model_dest: int32 [1024, 1], P('rows'), may hold values from 0 to 7; in each aligned block of 128 rows (0 to 127, 128 to 255, ...) at most 32 rows name the same one
- model_bus: int32 [1024], P('rows'), may hold values from 0 to 2047
- model_gain: float32 [1024], P('rows'), may hold values from 0.3 to 3
- model_lag: float32 [1024], P('rows'), may hold values from 0.1 to 0.9
- model_state: float32 [64, 1024], P('scen', 'rows'), may hold values from -6 to 6
- model_source: float32 [6, 64, 1024], P(None, 'scen', 'rows'), may hold values from -6 to 6
- switch_bus: int32 [2, 64, 4], P(None, 'scen'), may hold values from 0 to 4095, as said below
- switch_admittance: float32 [64, 4], P('scen'), may hold values from 0.5 to 4
Outputs:
- voltage: float32 [64, 16384], P('scen', 'rows')
- model_current: float32 [64, 1024], P('scen', 'rows')
The draws below stay inside these ranges and needn't reach their ends.
Inputs may be any that keep to these rules, and one draw needn't show every extreme that they name: `line_delay`: A line joins end (p, q * 2 + c) with end (q, p * 2 + c), with the same delay and impedance at both ends; no line joins the two devices of one subnetwork; delays of lines run from 2 to 4. `line_impedance`: equal at both ends of a line. `switch_bus`: the two buses of a switched branch differ. `inverse`: each block of 4096 columns is symmetric. `model_dest`: among the models of one index of rows at most 32 name the same index.
All inputs are finite; a program needn't handle non-finite values.
Results may differ from the reference program's by a relative error of at most 0.0024.
The reference program's roundings to bfloat16 on the way (of `feed`) count: a program that leaves them out, or rounds other values in their place, can miss the bound.
Values may be sent and summed in bfloat16 or wider, within the bound.
A program may use at most 128 MiB of HBM per device.

```python
import math
import jax
import jax.numpy as jnp
import numpy as np
from jax import lax

NSUB = 4096
MOD_DEV = 128
STEPS = 6
DMAX = 4
LINE_SLOTS = 2
ROWS_DEV = 2048
SUBS = 4
NB = 16384
SCEN = 64
NMOD = 1024
INJ_SLOTS = 32
N_ROWS = 8


def symmetric_pairs(values):
    places = jnp.arange(N_ROWS, dtype=jnp.int32)
    upper = places[:, None] < places[None, :]
    flipped = jnp.swapaxes(values, 0, 1)
    return jnp.where(upper[:, :, None], values, flipped)


def draw_line_delay(key, part):
    key_live, key_delay = jax.random.split(jax.random.fold_in(key, 11))
    live = jax.random.randint(key_live, (N_ROWS, N_ROWS, LINE_SLOTS), 0, 2)
    delays = jax.random.randint(key_delay, (N_ROWS, N_ROWS, LINE_SLOTS), 2, DMAX + 1)
    places = jnp.arange(N_ROWS, dtype=jnp.int32)
    apart = places[:, None] // 2 != places[None, :] // 2
    delays = jnp.where(apart[:, :, None] & (live == 1), delays, 0)
    delays = symmetric_pairs(delays)
    delays = delays.at[0, 2, 0].set(DMAX).at[2, 0, 0].set(DMAX)
    delays = delays.at[0, 2, 1].set(2).at[2, 0, 1].set(2)
    far_pair = places[None, :] == (places[:, None] + N_ROWS // 2) % N_ROWS
    slot_ids = jnp.arange(LINE_SLOTS, dtype=jnp.int32)
    far_delay = jnp.where(slot_ids == 0, 2, DMAX).astype(jnp.int32)
    delays = jnp.where(far_pair[:, :, None], far_delay[None, None, :], delays)
    return delays.reshape(N_ROWS, N_ROWS * LINE_SLOTS).astype(jnp.int32)


def draw_line_impedance(key, part):
    unit = jax.random.uniform(jax.random.fold_in(key, 23), (N_ROWS, N_ROWS, LINE_SLOTS), jnp.float32)
    values = 0.5 * jnp.exp(unit * math.log(4.0))
    values = symmetric_pairs(values)
    return values.reshape(N_ROWS, N_ROWS * LINE_SLOTS).astype(jnp.float32)


def draw_switch_bus(key, part):
    key_first, key_step = jax.random.split(jax.random.fold_in(key, 37))
    first = jax.random.randint(key_first, (SCEN, SUBS), 0, NSUB)
    offset = jax.random.randint(key_step, (SCEN, SUBS), 1, NSUB)
    second = (first + offset) % NSUB
    return jnp.stack([first, second]).astype(jnp.int32)


def draw_inverse(key, part):
    key_base, key_diag = jax.random.split(jax.random.fold_in(key, 5))
    places = jnp.arange(NSUB, dtype=jnp.int32)
    identity = (places[:, None] == places[None, :]).astype(jnp.float32)

    def one_block(g):
        base = jax.random.normal(jax.random.fold_in(key_base, g), (NSUB, NSUB), jnp.float32)
        coupling = (base + jnp.swapaxes(base, 0, 1)) * (0.3 / math.sqrt(2.0 * NSUB))
        diagonal = jax.random.uniform(jax.random.fold_in(key_diag, g), (NSUB,), jnp.float32, 1.0, 2.0)
        return (coupling + diagonal[:, None] * identity).astype(jnp.bfloat16)
    blocks = lax.map(one_block, jnp.arange(SUBS, dtype=jnp.int32))
    return jnp.transpose(blocks, (1, 0, 2)).reshape(NSUB, NB)


def set_ends(values, rng, least, largest):
    dims = values.shape
    spot = [jax.random.randint(jax.random.fold_in(rng, axis), (), 0, dims[axis]) for axis in range(len(dims))]
    values = values.at[tuple(spot)].set(least)
    longest = dims.index(max(dims))
    spot[longest] = (spot[longest] + 1) % dims[longest]
    return values.at[tuple(spot)].set(largest)


def shard_levels(stream_key, shape, cuts, least, largest):
    level, own = 1.0, jax.random.fold_in(stream_key, 6)
    for axis_at, parts in cuts:
        draws = jnp.exp(jax.random.uniform(jax.random.fold_in(own, axis_at), (parts,), jnp.float32, least / len(cuts), largest / len(cuts)))
        level = level * jnp.repeat(draws, shape[axis_at] // parts).reshape([-1 if axis == axis_at else 1 for axis in range(len(shape))])
    return level


def shared_out(key, own, number, rows, count, top, most, lean):
    order = jax.random.permutation(key, count)
    heavy_load, ordinary = shares(count, rows * top, most, lean, True), shares(count, rows * top, most, lean, False)
    places = jnp.arange(count)

    def named(tallies, offset_by):
        used = int((tallies > 0).sum())
        fixed = max(1, used // 4)
        shifted = fixed + (places - fixed + offset_by * (used - fixed)) % max(1, count - fixed)
        return jnp.zeros((count,), jnp.int32).at[order[jnp.where(places < fixed, places, shifted)]].set(jnp.asarray(tallies, jnp.int32))

    tallies = jnp.where(number % 4 == 0, named(heavy_load, number // 4), named(ordinary, number - number // 4 - 1))
    mixed = jax.random.permutation(jax.random.fold_in(own, 3), count)
    giver, receiver = mixed[0:count // 2 * 2:2], mixed[1:count // 2 * 2:2]
    room = jnp.minimum(tallies[giver] - 1, most - tallies[receiver]) // 2
    room = jnp.where((giver == order[0]) | (receiver == order[0]) | (tallies[receiver] == 0), 0, jnp.maximum(room, 0))
    shifted = jax.random.randint(jax.random.fold_in(own, 4), (count // 2,), 0, 1 << 20) % (room + 1)
    tallies = tallies.at[giver].add(-shifted).at[receiver].add(shifted)
    items = jnp.searchsorted(jnp.cumsum(tallies), jnp.arange(rows * top), side="right").astype(jnp.int32)
    table = items.reshape(top, rows).T
    table = table[jax.random.permutation(jax.random.fold_in(own, 1), rows)]
    offset_by = jax.random.randint(jax.random.fold_in(own, 2), (rows, 1), 0, top)
    return jnp.take_along_axis(table, (jnp.arange(top)[None, :] + offset_by) % top, axis=1)


def shares(amount, total, bound, skew, full):
    weights = [(1 << 20) // math.isqrt(rank ** skew) + 1 for rank in range(1, amount + 1)]
    largest = bound if full else min(bound, max(-(-total // amount), total * weights[0] // sum(weights)))
    least = 1 if total - largest >= amount - 1 else 0
    given, surplus = [largest] + [least] * (amount - 1), total - largest - least * (amount - 1)
    while surplus > 0:
        free = [i for i in range(1, amount) if given[i] < largest] or [i for i in range(1, amount) if given[i] < bound]
        pool, remaining = sum([weights[i] for i in free]), surplus
        for i in free:
            addition = min(bound - given[i], max(1, remaining * weights[i] // pool), surplus)
            given[i] = given[i] + addition
            surplus = surplus - addition
    return np.array(given)


def normal_values(stream_key, shape, spread, bound, cuts=(), held_as=jnp.bfloat16):
    values = spread * jax.random.normal(stream_key, shape, jnp.float32)
    if cuts:
        values = values * shard_levels(stream_key, shape, cuts, -0.22, 0.18)
    return jnp.clip(values, -bound, bound).astype(held_as)


def setup_inputs(seed: int = 0) -> dict:
    arg_keys = jax.random.split(jax.random.key(seed), 15)
    inverse = draw_inverse(jax.random.fold_in(arg_keys[14], 71), 0)
    voltage_prev = normal_values(arg_keys[1], (SCEN, NB), 1.0, 6.0, ((0, 4), (1, 8)), jnp.float32)
    line_delay = draw_line_delay(jax.random.fold_in(arg_keys[14], 71), 0)
    line_bus = set_ends(jax.random.randint(arg_keys[3], (N_ROWS, N_ROWS * LINE_SLOTS), 0, ROWS_DEV), jax.random.fold_in(arg_keys[3], 1), 0, ROWS_DEV - 1).astype(jnp.int32)
    line_impedance = draw_line_impedance(jax.random.fold_in(arg_keys[14], 71), 0)
    line_past = normal_values(arg_keys[5], (DMAX, 2, SCEN, N_ROWS, N_ROWS * LINE_SLOTS), 1.0, 6.0, ((2, 4), (3, 8)), jnp.float32)
    model_dest_keys = jax.random.split(jax.random.fold_in(arg_keys[6], 1), NMOD // MOD_DEV)
    model_dest_turns = jax.random.permutation(jax.random.fold_in(arg_keys[6], 3), NMOD // MOD_DEV)
    model_dest = jax.vmap(lambda own, number: shared_out(jax.random.fold_in(arg_keys[6], 2), own, number, MOD_DEV, N_ROWS, 1, INJ_SLOTS, 2))(model_dest_keys, model_dest_turns).reshape((NMOD, 1))
    model_bus = set_ends(jax.random.randint(arg_keys[7], (NMOD,), 0, ROWS_DEV), jax.random.fold_in(arg_keys[7], 1), 0, ROWS_DEV - 1).astype(jnp.int32)
    model_gain = jnp.clip(jnp.exp(math.log(3.0) - 2.3025851 * jax.random.uniform(arg_keys[8], (NMOD,), jnp.float32) ** shard_levels(arg_keys[8], (NMOD,), ((0, 8),), -0.2, 0.2)), 0.3, 3.0)
    model_lag = jnp.clip(0.1 + 0.79999997 * jax.random.uniform(arg_keys[9], (NMOD,), jnp.float32) ** shard_levels(arg_keys[9], (NMOD,), ((0, 8),), -0.2, 0.2), 0.1, 0.9)
    model_state = normal_values(arg_keys[10], (SCEN, NMOD), 1.0, 6.0, ((0, 4), (1, 8)), jnp.float32)
    model_source = normal_values(arg_keys[11], (STEPS, SCEN, NMOD), 1.0, 6.0, ((1, 4), (2, 8)), jnp.float32)
    switch_bus = draw_switch_bus(jax.random.fold_in(arg_keys[14], 71), 0)
    switch_admittance = jnp.clip(jnp.exp(math.log(4.0) - 2.0794415 * jax.random.uniform(arg_keys[13], (SCEN, SUBS), jnp.float32) ** shard_levels(arg_keys[13], (SCEN, SUBS), ((0, 4),), -0.2, 0.2)), 0.5, 4.0)
    return dict(inverse=inverse, voltage_prev=voltage_prev, line_delay=line_delay, line_bus=line_bus, line_impedance=line_impedance, line_past=line_past, model_dest=model_dest, model_bus=model_bus, model_gain=model_gain, model_lag=model_lag, model_state=model_state, model_source=model_source, switch_bus=switch_bus, switch_admittance=switch_admittance)


def solve_all(rhs, inv3):
    def one_sub(g):
        block = lax.dynamic_index_in_dim(inv3, g, axis=1, keepdims=False).astype(jnp.float32)
        part_rhs = lax.dynamic_index_in_dim(rhs, g, axis=1, keepdims=False)
        return jnp.dot(part_rhs, block, precision=lax.Precision.HIGHEST)
    result = lax.map(one_sub, jnp.arange(SUBS, dtype=jnp.int32))
    return jnp.swapaxes(result, 0, 1)


def reference(inverse, voltage_prev, line_delay, line_bus, line_impedance, line_past, model_dest, model_bus, model_gain, model_lag, model_state, model_source, switch_bus, switch_admittance):
    inv3 = inverse.reshape(NSUB, SUBS, NSUB)
    sub_ids = jnp.arange(SUBS, dtype=jnp.int32)[None, :]
    first = switch_bus[0]
    second = switch_bus[1]
    picked_first = jnp.transpose(inv3[:, sub_ids, first], (1, 2, 0)).astype(jnp.float32)
    picked_second = jnp.transpose(inv3[:, sub_ids, second], (1, 2, 0)).astype(jnp.float32)
    branch = picked_first - picked_second
    depth = jnp.take_along_axis(branch, first[:, :, None], axis=2)[:, :, 0] - jnp.take_along_axis(branch, second[:, :, None], axis=2)[:, :, 0]
    targets = (model_dest[:, 0] * ROWS_DEV + model_bus).astype(jnp.int32)
    end_index = (jnp.arange(N_ROWS, dtype=jnp.int32)[:, None] * ROWS_DEV + line_bus).astype(jnp.int32)
    history = [line_past[k] for k in range(DMAX)]
    volt = voltage_prev
    current = model_state
    for step in range(STEPS):
        seen = volt[:, targets]
        current = model_lag * current + (1.0 - model_lag) * model_gain * (model_source[step] - seen)
        feed = jnp.zeros((SCEN, NB), jnp.float32).at[:, targets].add(current)
        line_term = jnp.zeros((SCEN, N_ROWS, N_ROWS * LINE_SLOTS), jnp.float32)
        for delay in range(2, DMAX + 1):
            older = history[step - delay + DMAX]
            line_term = line_term + jnp.where(line_delay == delay, -(2.0 / line_impedance) * older[0] - older[1], 0.0)
        feed = feed.at[:, end_index].add(-line_term)
        rounded = feed.astype(jnp.bfloat16)
        rounded = lax.optimization_barrier(rounded)
        rhs = rounded.astype(jnp.float32).reshape(SCEN, SUBS, NSUB)
        base = solve_all(rhs, inv3)
        along = jnp.sum(rhs * branch, axis=2)
        factor = switch_admittance * along / (1.0 + switch_admittance * depth)
        volt = (base - factor[:, :, None] * branch).reshape(SCEN, NB)
        if step + 2 < STEPS:
            sent = jnp.stack([volt[:, end_index], line_term])
            sent = sent.reshape(2, SCEN, N_ROWS, N_ROWS, LINE_SLOTS)
            history.append(jnp.swapaxes(sent, 2, 3).reshape(2, SCEN, N_ROWS, N_ROWS * LINE_SLOTS))
    return volt, current
```

```python
import jax
import jax.numpy as jnp
from jax import lax
from jax.sharding import PartitionSpec as P


def swapped(value, axis, apart):
    mask = 2**apart
    pairs = [(source, source ^ mask) for source in range(lax.axis_size(axis))]
    return lax.ppermute(value, axis, pairs)


def slot_table(targets, sections, slots):
    onehot = (targets[:, None] == jnp.arange(sections, dtype=jnp.int32)[None, :]).astype(jnp.int32)
    count = targets.shape[0]
    earlier = jnp.arange(count, dtype=jnp.int32)[None, :] < jnp.arange(count, dtype=jnp.int32)[:, None]
    same = targets[:, None] == targets[None, :]
    rank = jnp.sum((earlier & same).astype(jnp.int32), axis=1)
    return targets * slots + rank


def exact_dot(left, right):
    return jnp.dot(left, right, precision=lax.Precision.HIGHEST)


def per_device(
    inverse,
    voltage_prev,
    line_delay,
    line_bus,
    line_impedance,
    line_past,
    model_dest,
    model_bus,
    model_gain,
    model_lag,
    model_state,
    model_source,
    switch_bus,
    switch_admittance,
):
    n = lax.axis_size("rows")
    groups = lax.axis_size("scen")
    place = lax.axis_index("rows")
    share = lax.axis_index("scen")
    subnet = place // 2
    half = place % 2
    lower = half == 0
    depth_rows, width = inverse.shape
    scen = voltage_prev.shape[0]
    steps = model_source.shape[0]
    ends = line_bus.shape[1]
    models = model_bus.shape[0]
    depth_max = line_past.shape[0]
    slots = max(2, 2 * models // n)
    cap = n * slots
    f32, bf16 = jnp.float32, jnp.bfloat16

    def by_half(own, other):
        return jnp.where(lower, jnp.concatenate([own, other], -1), jnp.concatenate([other, own], -1))

    slot = slot_table(model_dest[:, 0], n, slots)
    placing = (slot[:, None] == jnp.arange(cap, dtype=jnp.int32)[None, :]).astype(f32)
    bus_out = exact_dot((model_bus + 1).astype(f32)[None], placing)
    bus_out = jnp.broadcast_to(bus_out.reshape(n // 2, 1, 2 * slots), (n // 2, 2, 2 * slots)).reshape(n, 2 * slots)
    ends_out = jnp.broadcast_to(line_bus.astype(f32) + 1.0, (n, ends))
    buses = lax.all_to_all(jnp.concatenate([bus_out, ends_out], 1), "rows", 0, 0, tiled=True)
    model_pts = buses[:, : 2 * slots].reshape(n, 2, slots).transpose(1, 0, 2).reshape(2, cap)
    ends_pts = lax.dynamic_slice_in_dim(buses[:, 2 * slots :], subnet * 2, 2, axis=0)
    half_pts = jnp.concatenate([model_pts, ends_pts], 1).astype(jnp.int32) - 1
    pts = jnp.where(half_pts < 0, -1, half_pts + jnp.array([[0], [width]], jnp.int32)).reshape(-1)
    own_pts = lax.dynamic_index_in_dim(half_pts, half, 0, keepdims=False)
    hp = cap + ends

    payload = jnp.concatenate(
        [
            model_lag[None],
            ((1.0 - model_lag) * model_gain)[None],
            model_state,
            model_source.reshape(steps * scen, models),
        ],
        0,
    )
    sent = exact_dot(payload, placing).reshape(-1, n // 2, 1, 2 * slots)
    sent = jnp.broadcast_to(sent, (payload.shape[0], n // 2, 2, 2 * slots)).reshape(-1, n, 2 * slots).transpose(1, 0, 2)
    got = lax.all_to_all(sent, "rows", 0, 0, tiled=True)
    got = got.reshape(n, -1, 2, slots).transpose(1, 2, 0, 3).reshape(-1, 2, cap)
    zeros_ends = jnp.zeros((got.shape[0], 2, ends), f32)
    got = jnp.concatenate([got, zeros_ends], 2).reshape(-1, 2 * hp)
    lag, gain, current = got[0], got[1], got[2 : 2 + scen]
    source = got[2 + scen :].reshape(steps, scen, 2 * hp)

    col_sel = (jnp.arange(width, dtype=jnp.int32)[:, None] == own_pts[None, :]).astype(bf16)
    first_all = lax.dynamic_index_in_dim(lax.all_gather(switch_bus[0], "scen", axis=0, tiled=True), subnet, 1, keepdims=False)
    second_all = lax.dynamic_index_in_dim(lax.all_gather(switch_bus[1], "scen", axis=0, tiled=True), subnet, 1, keepdims=False)
    row_ids = jnp.arange(depth_rows, dtype=jnp.int32)[None, :] + share * depth_rows
    col_ids = jnp.arange(width, dtype=jnp.int32)[None, :] + half * width
    picks = (row_ids == first_all[:, None]).astype(bf16) - (row_ids == second_all[:, None]).astype(bf16)
    col_picks = (col_ids == first_all[:, None]).astype(f32) - (col_ids == second_all[:, None]).astype(f32)
    row_sel = (row_ids == pts[:, None]).astype(bf16)
    narrow = jnp.dot(inverse, col_sel, preferred_element_type=f32).astype(bf16)
    part = jnp.dot(row_sel, narrow, preferred_element_type=f32).astype(bf16)
    own_cols = lax.psum(part, "scen")
    branch_part = jnp.dot(picks, inverse, preferred_element_type=f32)
    pts_part = jnp.dot(picks, narrow, preferred_element_type=f32)
    depth_part = jnp.sum(branch_part * col_picks, axis=1, keepdims=True)
    side = lax.psum(jnp.concatenate([pts_part, depth_part], 1), "scen")
    side = lax.dynamic_slice_in_dim(side, share * scen, scen, axis=0)

    own_diag = lax.dynamic_slice_in_dim(own_cols, half * hp, hp, axis=0)
    cross = lax.dynamic_slice_in_dim(own_cols, (1 - half) * hp, hp, axis=0).T
    other_diag = swapped(own_diag, "rows", 0)
    other_cols = jnp.where(lower, jnp.concatenate([cross, other_diag], 0), jnp.concatenate([other_diag, cross], 0))
    matrix = by_half(own_cols, other_cols)

    volt0 = exact_dot(voltage_prev, col_sel.astype(f32))
    past = line_past[:, :, :, 0, :].reshape(depth_max * 2 * scen, ends)
    line_info = jnp.concatenate([past, line_delay.astype(f32), line_impedance], 0)
    other_side = swapped(side, "rows", 0)
    other_volt = swapped(volt0, "rows", 0)
    other_info = swapped(line_info, "rows", 0)
    depth = (side + other_side)[:, hp]
    branch = by_half(side[:, :hp], other_side[:, :hp])
    volt = by_half(volt0, other_volt)
    info = jnp.stack([line_info, other_info])
    info = jnp.where(lower, info, info[::-1])
    past = info[:, : depth_max * 2 * scen].reshape(2, depth_max, 2, scen, ends)
    history = [past[:, k] for k in range(depth_max)]
    delays = info[:, -2][:, None, :]
    impedance = info[:, -1][:, None, :]
    admit = lax.dynamic_index_in_dim(switch_admittance, subnet, axis=1, keepdims=False)

    same = pts[:, None] == pts[None, :]
    before = jnp.arange(2 * hp, dtype=jnp.int32)[:, None] < jnp.arange(2 * hp, dtype=jnp.int32)[None, :]
    leading = jnp.sum((same & before).astype(jnp.int32), axis=0) == 0
    merge = (same & leading[None, :]).astype(f32)

    for step in range(steps):
        current = lag * current + gain * (source[step] - volt)
        line_term = jnp.zeros((2, scen, ends), f32)
        for delay in range(2, depth_max + 1):
            older = history[step - delay + depth_max]
            line_term = line_term + jnp.where(
                delays == delay, -(2.0 / impedance) * older[:, 0] - older[:, 1], 0.0
            )
        zeros = jnp.zeros((scen, cap), f32)
        lines = jnp.concatenate([zeros, line_term[0], zeros, line_term[1]], 1)
        rhs = exact_dot(current - lines, merge).astype(bf16)
        along = jnp.sum(rhs.astype(f32) * branch, axis=1)
        factor = admit * along / (1.0 + admit * depth)
        if step + 1 < steps:
            base = jnp.dot(rhs, matrix, preferred_element_type=f32)
            volt = base - factor[:, None] * branch
        if step + 2 < steps:
            own_volt = jnp.where(lower, volt[:, cap:hp], volt[:, hp + cap :])
            own_term = jnp.where(lower, line_term[0], line_term[1])
            out = jnp.stack([own_volt, own_term]).reshape(2, scen, n // 2, 2 * ends // n)
            out = jnp.broadcast_to(out.transpose(2, 0, 1, 3)[:, None], (n // 2, 2, 2, scen, 2 * ends // n))
            back = lax.all_to_all(out.reshape(n, 2, scen, 2 * ends // n), "rows", 0, 0, tiled=True)
            back = back.reshape(n, 2, scen, 2, ends // n).transpose(3, 1, 2, 0, 4)
            history.append(back.reshape(2, 2, scen, ends))

    rhs_all = lax.all_gather(rhs, "scen", axis=0, tiled=True)
    factor_all = lax.all_gather(factor[:, None], "scen", axis=0, tiled=True)
    dense = jnp.dot(rhs_all, row_sel, preferred_element_type=f32).astype(bf16)
    partial = jnp.dot(dense, inverse, preferred_element_type=f32) - factor_all * branch_part
    voltage = lax.psum_scatter(partial, "scen", scatter_dimension=0, tiled=True)

    own_current = jnp.where(lower, current[:, :cap], current[:, hp : hp + cap])
    back = lax.all_to_all(own_current.reshape(scen, n, slots).transpose(1, 0, 2), "rows", 0, 0, tiled=True)
    model_current = lax.dot_general(
        back.transpose(1, 0, 2).reshape(scen, cap), placing, (((1,), (1,)), ((), ())), precision=lax.Precision.HIGHEST
    )
    return (voltage, model_current)


def solution(mesh):
    placed = (
        P("scen", "rows"),
        P("scen", "rows"),
        P("rows", None),
        P("rows", None),
        P("rows", None),
        P(None, None, "scen", "rows", None),
        P("rows", None),
        P("rows"),
        P("rows"),
        P("rows"),
        P("scen", "rows"),
        P(None, "scen", "rows"),
        P(None, "scen", None),
        P("scen", None),
    )
    return jax.shard_map(
        per_device,
        mesh=mesh,
        in_specs=placed,
        out_specs=(P("scen", "rows"), P("scen", "rows")),
        check_vma=False,
    )
```

```python
import functools

import jax
import jax.numpy as jnp
from jax import lax
from jax.experimental import pallas as pl
from jax.experimental.pallas import tpu as pltpu
from jax.sharding import PartitionSpec as P


def slot_table(targets, sections, slots):
    onehot = (targets[:, None] == jnp.arange(sections, dtype=jnp.int32)[None, :]).astype(jnp.int32)
    count = targets.shape[0]
    earlier = jnp.arange(count, dtype=jnp.int32)[None, :] < jnp.arange(count, dtype=jnp.int32)[:, None]
    same = targets[:, None] == targets[None, :]
    rank = jnp.sum((earlier & same).astype(jnp.int32), axis=1)
    return targets * slots + rank


def exact_dot(left, right):
    return jnp.dot(left, right, precision=lax.Precision.HIGHEST)


def split_dot(value, selector):
    rows = value.shape[0]
    high = value.astype(jnp.bfloat16)
    rest = value - high.astype(jnp.float32)
    middle = rest.astype(jnp.bfloat16)
    low = (rest - middle.astype(jnp.float32)).astype(jnp.bfloat16)
    stacked = jnp.concatenate([high, middle, low], 0)
    out = jnp.dot(stacked, selector, preferred_element_type=jnp.float32)
    return out[:rows] + out[rows : 2 * rows] + out[2 * rows :]


def step_kernel(
    n,
    groups,
    steps,
    depth_max,
    cap,
    part_ref,
    side_ref,
    volt_ref,
    info_ref,
    rates_ref,
    state_ref,
    source_ref,
    merge_ref,
    row_sel_ref,
    perm_ref,
    end_sub_ref,
    admit_ref,
    inverse_ref,
    branch_part_ref,
    home_ref,
    voltage_ref,
    current_ref,
    part_in,
    side_in,
    matrix,
    volt_in,
    info_in,
    line_out,
    line_in,
    feed_out,
    feed_in,
    factor_out,
    factor_in,
    partial_out,
    partial_in,
    state_out,
    state_in,
    group_sems,
    pair_sems,
    line_sems,
    last_sems,
    home_sems,
):
    f32, bf16 = jnp.float32, jnp.bfloat16
    place = lax.axis_index("rows")
    share = lax.axis_index("scen")
    subs = n // 2
    subnet, half = place // 2, place % 2
    base_row = subnet * 2
    size = 2 * groups
    me = half * groups + share
    scen = state_ref.shape[0]
    points = matrix.shape[0]
    block = points // size
    lower = half == 0

    def member(index):
        return (base_row + index // groups, index % groups)

    def remote(src, dst, sems, device):
        return pltpu.make_async_remote_copy(
            src_ref=src,
            dst_ref=dst,
            send_sem=sems.at[0],
            recv_sem=sems.at[1],
            device_id=device,
            device_id_type=pl.DeviceIdType.MESH,
        )

    barrier = pltpu.get_barrier_semaphore()
    for d in range(1, size):
        pl.semaphore_signal(
            barrier, inc=1, device_id=member((me + d) % size), device_id_type=pl.DeviceIdType.MESH
        )
    for d in range(1, subs):
        for other in range(2):
            device = (((subnet + d) % subs) * 2 + other, share)
            pl.semaphore_signal(barrier, inc=1, device_id=device, device_id_type=pl.DeviceIdType.MESH)
    pl.semaphore_wait(barrier, size - 1 + 2 * (subs - 1))

    first = []
    for d in range(1, size):
        peer = (me + d) % size
        rows = pl.ds(pl.multiple_of(peer * block, 16), block)
        first.append(remote(part_ref.at[rows], part_in.at[d - 1], group_sems.at[0, d], member(peer)))
    for copy in first:
        copy.start()
    pair = ((place // 2) * 2 + (1 - half), share)
    pairs = [
        remote(volt_ref, volt_in, pair_sems.at[0], pair),
        remote(info_ref, info_in, pair_sems.at[1], pair),
    ]
    for copy in pairs:
        copy.start()
    sides = []
    for d in range(1, size):
        peer = (me + d) % size
        rows = pl.ds(pl.multiple_of((peer % groups) * scen, 8), scen)
        sides.append(remote(side_ref.at[rows], side_in.at[d - 1], group_sems.at[1, d], member(peer)))
    for copy in sides:
        copy.start()
    own_rows = pl.ds(pl.multiple_of(me * block, 16), block)

    def placed(pieces):
        lows = jnp.zeros_like(pieces[0][1][:, :cap])
        highs = jnp.zeros_like(lows)
        rest = jnp.zeros_like(pieces[0][1][:, cap:])
        for from_lower, piece in pieces:
            lows = lows + jnp.where(from_lower, piece[:, :cap], 0.0)
            highs = highs + jnp.where(from_lower, 0.0, piece[:, :cap])
            rest = rest + piece[:, cap:]
        return lows, highs, rest

    pieces = [(lower, part_ref[own_rows, :].astype(f32))]
    for d in range(1, size):
        first[d - 1].wait()
        pieces.append(((me + size - d) % size < groups, part_in[d - 1].astype(f32)))
    matrix[own_rows, :] = jnp.concatenate(placed(pieces), 1).astype(bf16)
    second = []
    for d in range(1, size):
        second.append(
            remote(matrix.at[own_rows], matrix.at[own_rows], group_sems.at[2, d], member((me + d) % size))
        )
    for copy in second:
        copy.start()

    pieces = [(lower, side_ref[pl.ds(pl.multiple_of(share * scen, 8), scen), :])]
    for d in range(1, size):
        sides[d - 1].wait()
        pieces.append(((me + size - d) % size < groups, side_in[d - 1]))
    lows, highs, rest = placed(pieces)
    ends = perm_ref.shape[0]
    branch = jnp.concatenate([lows, highs, rest[:, :ends]], 1)
    depth = rest[:, ends : ends + 1]
    for copy in pairs:
        copy.wait()
    own_volt, other_volt = volt_ref[...], volt_in[...]
    volt = jnp.concatenate(
        [jnp.where(lower, own_volt, other_volt), jnp.where(lower, other_volt, own_volt)], 1
    )
    past_rows = depth_max * 2 * scen
    info = info_ref[...] + info_in[...]
    delays = info[past_rows : past_rows + 1]
    impedance = info[past_rows + 1 : past_rows + 2]
    admittance = 2.0 / jnp.where(delays == 0.0, 1.0, impedance)
    history = [info[k * 2 * scen : (k + 1) * 2 * scen] for k in range(depth_max)]
    lag, gain = rates_ref[0:1, :], rates_ref[1:2, :]
    admit = admit_ref[:, 0:1]
    current = state_ref[...]
    lines = []
    homes = []
    for step in range(steps):
        current = lag * current + gain * (source_ref[step] - volt)
        if step + 1 == steps:
            state_out[...] = jnp.where(lower, current[:, :cap], current[:, cap:])
            for d in range(1, n):
                homes.append(
                    remote(state_out, state_in.at[d - 1], home_sems.at[d], ((place + d) % n, share))
                )
            for copy in homes:
                copy.start()
        if step >= 2:
            for copy in lines[step - 2]:
                copy.wait()
            merged = jnp.zeros((2 * scen, ends), f32)
            for d in range(1, subs):
                moved = split_dot(line_in[step - 2, d - 1], perm_ref[...])
                merged = merged + jnp.where(end_sub_ref[0:1, :] == (subnet + subs - d) % subs, moved, 0.0)
            history.append(merged)
        line_term = jnp.zeros((scen, ends), f32)
        for delay in range(2, depth_max + 1):
            older = history[step - delay + depth_max]
            line_term = line_term + jnp.where(
                delays == delay, -admittance * older[:scen] - older[scen:], 0.0
            )
        feed = split_dot(jnp.concatenate([current, -line_term], 1), merge_ref[...])
        rhs = feed.astype(bf16)
        along = jnp.sum(rhs.astype(f32) * branch, axis=1, keepdims=True)
        factor = admit * along / (1.0 + admit * depth)
        if step == 0:
            for copy in second:
                copy.wait()
        if step + 1 < steps:
            full = jnp.dot(rhs, matrix[...], preferred_element_type=f32) - factor * branch
            volt = full[:, : 2 * cap]
        if step + 2 < steps:
            line_out[step] = jnp.concatenate([full[:, 2 * cap :], line_term], 0)
            lines.append(
                [
                    remote(
                        line_out.at[step],
                        line_in.at[step, d - 1],
                        line_sems.at[step, d],
                        (((subnet + d) % subs) * 2 + half, share),
                    )
                    for d in range(1, subs)
                ]
            )
            for copy in lines[step]:
                copy.start()

    feed_out[...] = rhs
    factor_out[...] = jnp.broadcast_to(factor, factor_out.shape)
    shared = []
    for d in range(1, groups):
        device = (place, (share + d) % groups)
        shared.append(remote(feed_out, feed_in.at[d - 1], last_sems.at[0, d], device))
        shared.append(remote(factor_out, factor_in.at[d - 1], last_sems.at[1, d], device))
    for copy in shared:
        copy.start()
    for copy in shared:
        copy.wait()
    feeds = jnp.concatenate([feed_in[d - 1] for d in range(1, groups)] + [rhs], 0)
    dense = jnp.dot(feeds, row_sel_ref[...], preferred_element_type=f32).astype(bf16)
    width = inverse_ref.shape[1]
    tile = min(width, 512)
    for at in range(0, width, tile):
        product = jnp.dot(dense, inverse_ref[:, at : at + tile], preferred_element_type=f32)
        for d in range(1, groups):
            rows = pl.ds(pl.multiple_of(((share + groups - d) % groups) * scen, 8), scen)
            partial_out[d - 1, :, at : at + tile] = (
                product[(d - 1) * scen : d * scen]
                - factor_in[d - 1][:, 0:1] * branch_part_ref[rows, at : at + tile]
            )
        rows = pl.ds(pl.multiple_of(share * scen, 8), scen)
        voltage_ref[:, at : at + tile] = (
            product[(groups - 1) * scen :] - factor * branch_part_ref[rows, at : at + tile]
        )
    partials = []
    for d in range(1, groups):
        device = (place, (share + groups - d) % groups)
        partials.append(remote(partial_out.at[d - 1], partial_in.at[d - 1], last_sems.at[2, d], device))
    for copy in partials:
        copy.start()
    for copy in homes:
        copy.wait()
    out = split_dot(state_out[...], home_ref[0])
    for d in range(1, n):
        out = out + split_dot(state_in[d - 1], home_ref[d])
    current_ref[...] = out
    for copy in partials:
        copy.wait()
    total = voltage_ref[...]
    for d in range(1, groups):
        total = total + partial_in[d - 1]
    voltage_ref[...] = total


def per_device(
    inverse,
    voltage_prev,
    line_delay,
    line_bus,
    line_impedance,
    line_past,
    model_dest,
    model_bus,
    model_gain,
    model_lag,
    model_state,
    model_source,
    switch_bus,
    switch_admittance,
):
    n = lax.axis_size("rows")
    groups = lax.axis_size("scen")
    place = lax.axis_index("rows")
    share = lax.axis_index("scen")
    subnet = place // 2
    half = place % 2
    lower = half == 0
    depth_rows, width = inverse.shape
    scen = voltage_prev.shape[0]
    steps = model_source.shape[0]
    ends = line_bus.shape[1]
    models = model_bus.shape[0]
    depth_max = line_past.shape[0]
    slots = max(2, 2 * models // n)
    cap = n * slots
    f32, bf16 = jnp.float32, jnp.bfloat16

    pad = max(128, 2 * ends)
    points = 2 * cap + pad

    def end_lanes(values):
        none = jnp.zeros((values.shape[0], ends), values.dtype)
        both = jnp.where(
            lower, jnp.concatenate([values, none], 1), jnp.concatenate([none, values], 1)
        )
        return jnp.pad(both, ((0, 0), (0, pad - 2 * ends)))

    slot = slot_table(model_dest[:, 0], n, slots)
    placing = (slot[:, None] == jnp.arange(cap, dtype=jnp.int32)[None, :]).astype(f32)
    bus_out = exact_dot((model_bus + 1).astype(f32)[None], placing)
    bus_out = jnp.broadcast_to(bus_out.reshape(n // 2, 1, 2 * slots), (n // 2, 2, 2 * slots)).reshape(n, 2 * slots)
    ends_out = jnp.broadcast_to(line_bus.astype(f32) + 1.0, (n, ends))
    buses = lax.all_to_all(jnp.concatenate([bus_out, ends_out], 1), "rows", 0, 0, tiled=True)
    model_pts = buses[:, : 2 * slots].reshape(n, 2, slots).transpose(1, 0, 2).reshape(2, cap)
    ends_pts = lax.dynamic_slice_in_dim(buses[:, 2 * slots :], subnet * 2, 2, axis=0)
    model_pts = model_pts.astype(jnp.int32) - 1
    ends_pts = ends_pts.astype(jnp.int32) - 1
    shift = jnp.array([[0], [width]], jnp.int32)
    pts = jnp.concatenate(
        [
            jnp.where(model_pts < 0, -1, model_pts + shift).reshape(-1),
            (ends_pts + shift).reshape(-1),
            jnp.full((pad - 2 * ends,), -1, jnp.int32),
        ]
    )
    own_models = lax.dynamic_index_in_dim(model_pts, half, 0, keepdims=False)
    own_pts = jnp.concatenate([own_models, end_lanes(line_bus + 1)[0] - 1])

    payload = jnp.concatenate(
        [
            model_lag[None],
            ((1.0 - model_lag) * model_gain)[None],
            jnp.zeros((6, models), f32),
            model_state,
            model_source.reshape(steps * scen, models),
        ],
        0,
    )
    count = payload.shape[0]
    sent = exact_dot(payload, placing).reshape(-1, n // 2, 1, 2 * slots)
    sent = jnp.broadcast_to(sent, (count, n // 2, 2, 2 * slots)).reshape(-1, n, 2 * slots).transpose(1, 0, 2)
    got = lax.all_to_all(sent, "rows", 0, 0, tiled=True)
    got = got.reshape(n, -1, 2, slots).transpose(1, 2, 0, 3).reshape(-1, 2 * cap)
    rates, state = got[:8], got[8 : 8 + scen]
    source = got[8 + scen :].reshape(steps, scen, 2 * cap)

    col_sel = (jnp.arange(width, dtype=jnp.int32)[:, None] == own_pts[None, :]).astype(bf16)
    switches = lax.all_gather(switch_bus, "scen", axis=1, tiled=True)
    switches = lax.dynamic_index_in_dim(switches, subnet, 2, keepdims=False)
    row_ids = jnp.arange(depth_rows, dtype=jnp.int32)[None, :] + share * depth_rows
    col_ids = jnp.arange(width, dtype=jnp.int32)[None, :] + half * width
    picks = (row_ids == switches[0][:, None]).astype(bf16) - (row_ids == switches[1][:, None]).astype(bf16)
    col_picks = (col_ids == switches[0][:, None]).astype(f32) - (col_ids == switches[1][:, None]).astype(f32)
    row_sel = (row_ids == pts[:, None]).astype(bf16)
    narrow = jnp.dot(inverse, col_sel, preferred_element_type=f32).astype(bf16)
    part = jnp.dot(row_sel, narrow, preferred_element_type=f32).astype(bf16)
    branch_part = jnp.dot(picks, inverse, preferred_element_type=f32)
    pts_part = jnp.dot(picks, narrow, preferred_element_type=f32)
    depth_part = jnp.sum(branch_part * col_picks, axis=1, keepdims=True)
    side = jnp.concatenate([pts_part, jnp.broadcast_to(depth_part, (depth_part.shape[0], 128))], 1)
    volt0 = exact_dot(voltage_prev, col_sel[:, :cap].astype(f32))
    past = line_past[:, :, :, 0, :].reshape(depth_max * 2 * scen, ends)
    info = end_lanes(
        jnp.concatenate([past, line_delay.astype(f32), line_impedance, jnp.zeros((6, ends), f32)], 0)
    )
    same = pts[:, None] == pts[None, :]
    before = jnp.arange(points, dtype=jnp.int32)[:, None] < jnp.arange(points, dtype=jnp.int32)[None, :]
    leading = jnp.sum((same & before).astype(jnp.int32), axis=0) == 0
    merge = (same & leading[None, :]).astype(bf16)

    per_pair = ends // n
    lane = jnp.arange(pad, dtype=jnp.int32)
    lane_half, slot_at = lane // ends, lane % ends
    partner = slot_at // per_pair
    origin = (partner % 2) * ends + (2 * subnet + lane_half) * per_pair + slot_at % per_pair
    perm = ((jnp.arange(pad, dtype=jnp.int32)[:, None] == origin[None, :]) & (lane < 2 * ends)[None, :]).astype(bf16)
    end_sub = jnp.broadcast_to((partner // 2)[None], (8, pad))
    admit = lax.dynamic_index_in_dim(switch_admittance, subnet, axis=1, keepdims=False)
    admit = jnp.broadcast_to(admit[:, None], (scen, 128))
    rank = slot % slots
    target = (place - jnp.arange(n, dtype=jnp.int32)) % n
    home = (
        (model_dest[:, 0][None, None, :] == target[:, None, None])
        & (jnp.arange(cap, dtype=jnp.int32)[None, :, None] == (place * slots + rank)[None, None, :])
    ).astype(bf16)

    size = 2 * groups
    cols = cap + pad
    vmem = pl.BlockSpec(memory_space=pltpu.VMEM)
    voltage, model_current = pl.pallas_call(
        functools.partial(step_kernel, n, groups, steps, depth_max, cap),
        out_shape=(
            jax.ShapeDtypeStruct((scen, width), f32),
            jax.ShapeDtypeStruct((scen, models), f32),
        ),
        in_specs=[vmem] * 15,
        out_specs=(vmem, vmem),
        scratch_shapes=[
            pltpu.VMEM((size - 1, points // size, cols), bf16),
            pltpu.VMEM((size - 1, scen, cols + 128), f32),
            pltpu.VMEM((points, points), bf16),
            pltpu.VMEM((scen, cap), f32),
            pltpu.VMEM(info.shape, f32),
            pltpu.VMEM((steps - 2, 2 * scen, pad), f32),
            pltpu.VMEM((steps - 2, n // 2 - 1, 2 * scen, pad), f32),
            pltpu.VMEM((scen, points), bf16),
            pltpu.VMEM((groups - 1, scen, points), bf16),
            pltpu.VMEM((scen, 128), f32),
            pltpu.VMEM((groups - 1, scen, 128), f32),
            pltpu.VMEM((groups - 1, scen, width), f32),
            pltpu.VMEM((groups - 1, scen, width), f32),
            pltpu.VMEM((scen, cap), f32),
            pltpu.VMEM((n - 1, scen, cap), f32),
            pltpu.SemaphoreType.DMA((3, size, 2)),
            pltpu.SemaphoreType.DMA((2, 2)),
            pltpu.SemaphoreType.DMA((steps - 2, n // 2, 2)),
            pltpu.SemaphoreType.DMA((3, groups, 2)),
            pltpu.SemaphoreType.DMA((n, 2)),
        ],
        compiler_params=pltpu.CompilerParams(
            collective_id=0, has_side_effects=True, vmem_limit_bytes=56 * 2**20
        ),
    )(
        part, side, volt0, info, rates, state, source, merge, row_sel, perm, end_sub, admit,
        inverse, branch_part, home,
    )
    return (voltage, model_current)


def solution(mesh):
    placed = (
        P("scen", "rows"),
        P("scen", "rows"),
        P("rows", None),
        P("rows", None),
        P("rows", None),
        P(None, None, "scen", "rows", None),
        P("rows", None),
        P("rows"),
        P("rows"),
        P("rows"),
        P("scen", "rows"),
        P(None, "scen", "rows"),
        P(None, "scen", None),
        P("scen", None),
    )
    return jax.shard_map(
        per_device,
        mesh=mesh,
        in_specs=placed,
        out_specs=(P("scen", "rows"), P("scen", "rows")),
        check_vma=False,
    )
```

```python
import functools

import jax
import jax.numpy as jnp
import numpy as np
from jax import lax
from jax.experimental import pallas as pl
from jax.experimental.pallas import tpu as pltpu
from jax.sharding import PartitionSpec as P


def split_dot(value, selector):
    rows = value.shape[0]
    high = value.astype(jnp.bfloat16)
    rest = value - high.astype(jnp.float32)
    middle = rest.astype(jnp.bfloat16)
    low = (rest - middle.astype(jnp.float32)).astype(jnp.bfloat16)
    stacked = jnp.concatenate([high, middle, low], 0)
    out = jnp.dot(stacked, selector, preferred_element_type=jnp.float32)
    return out[:rows] + out[rows : 2 * rows] + out[2 * rows :]


def step_kernel(
    n,
    groups,
    steps,
    depth_max,
    cap,
    slots,
    inverse_ref,
    prev_ref,
    meta_ref,
    state_ref,
    source_ref,
    info_ref,
    switch_ref,
    order_ref,
    lanes_ref,
    voltage_ref,
    current_ref,
    bus_out,
    bus_in,
    switch_in,
    model_out,
    model_in,
    col_sel,
    row_sel,
    narrow,
    merge,
    branch_part,
    part,
    side,
    volt_out,
    part_in,
    side_in,
    matrix,
    volt_in,
    info_in,
    line_out,
    line_in,
    feed_out,
    feed_in,
    factor_out,
    factor_in,
    partial_out,
    partial_in,
    state_out,
    state_in,
    group_sems,
    pair_sems,
    line_sems,
    last_sems,
    home_sems,
    bus_sems,
    model_sems,
    switch_sems,
):
    f32, bf16 = jnp.float32, jnp.bfloat16
    place = lax.axis_index("rows")
    share = lax.axis_index("scen")
    subs = n // 2
    subnet, half = place // 2, place % 2
    base_row = subnet * 2
    size = 2 * groups
    me = half * groups + share
    scen = state_ref.shape[0]
    points = matrix.shape[0]
    block = points // size
    lower = half == 0

    def member(index):
        return (base_row + index // groups, index % groups)

    def remote(src, dst, sems, device):
        return pltpu.make_async_remote_copy(
            src_ref=src,
            dst_ref=dst,
            send_sem=sems.at[0],
            recv_sem=sems.at[1],
            device_id=device,
            device_id_type=pl.DeviceIdType.MESH,
        )

    barrier = pltpu.get_barrier_semaphore()
    for d in range(1, size):
        pl.semaphore_signal(
            barrier, inc=1, device_id=member((me + d) % size), device_id_type=pl.DeviceIdType.MESH
        )
    for d in range(1, subs):
        for other in range(2):
            device = (((subnet + d) % subs) * 2 + other, share)
            pl.semaphore_signal(barrier, inc=1, device_id=device, device_id_type=pl.DeviceIdType.MESH)
    pl.semaphore_wait(barrier, size - 1 + 2 * (subs - 1))

    width = inverse_ref.shape[1]
    local = inverse_ref.shape[0]
    models = meta_ref.shape[1]
    ends = lanes_ref.shape[1]
    per_group = 128 // (2 * slots)
    past_rows = depth_max * 2 * scen
    iota = functools.partial(lax.broadcasted_iota, jnp.int32)
    dest = jnp.broadcast_to(meta_ref[0:1, :], (models, models))
    dest_col = dest.T
    same = dest == dest_col
    rows_at, lanes_at = iota((models, models), 0), iota((models, models), 1)
    rank_col = jnp.sum(jnp.where(same & (lanes_at < rows_at), 1.0, 0.0), axis=1, keepdims=True)
    rank_row = jnp.sum(jnp.where(same & (rows_at < lanes_at), 1.0, 0.0), axis=0, keepdims=True)
    dest_col = dest_col[:, 0:1].astype(jnp.int32)
    spot = (dest_col >> 1) * 128 + (dest_col & 1) * slots + rank_col.astype(jnp.int32)
    spot = spot + (place % per_group) * (2 * slots)
    placing = jnp.where(iota((models, subs * 128), 1) == spot, 1.0, 0.0).astype(bf16)
    dest_row = meta_ref[0:1, :].astype(jnp.int32)
    bus_row = meta_ref[1:2, :] + ((dest_row & 1) * width + 1).astype(f32)
    spread = split_dot(jnp.broadcast_to(bus_row, (16, models)), placing)
    for g in range(subs):
        bus_out[g] = spread[:, g * 128 : (g + 1) * 128]
    moved_buses, moved_models = [], []
    for d in range(1, n):
        to = (place + d) % n
        moved_buses.append(remote(bus_out.at[to // 2], bus_in.at[place], bus_sems.at[d], (to, share)))
    for copy in moved_buses:
        copy.start()
    bus_in[place] = bus_out[subnet]
    pair = ((place // 2) * 2 + (1 - half), share)
    info_copy = remote(info_ref, info_in, pair_sems.at[1], pair)
    info_copy.start()
    switches = []
    for d in range(1, groups):
        device = (place, (share + d) % groups)
        switches.append(remote(switch_ref, switch_in.at[d - 1], switch_sems.at[d], device))
    for copy in switches:
        copy.start()
    lag_row = meta_ref[2:3, :]
    gain_row = (1.0 - lag_row) * meta_ref[3:4, :]
    payload = jnp.concatenate(
        [
            jnp.broadcast_to(lag_row, (8, models)),
            jnp.broadcast_to(gain_row, (8, models)),
            state_ref[...],
            source_ref[...],
        ],
        0,
    )
    for g in range(subs):
        model_out[g] = split_dot(payload, placing[:, g * 128 : (g + 1) * 128])
    for d in range(1, n):
        to = (place + d) % n
        moved_models.append(remote(model_out.at[to // 2], model_in.at[place], model_sems.at[d], (to, share)))

    for copy in switches:
        copy.wait()
    blocks = [switch_in[d - 1] for d in range(1, groups)] + [switch_ref[...]]
    scens = groups * scen
    pick_at = jnp.concatenate(blocks, 0).astype(jnp.int32)
    pick_a, pick_b = pick_at[:, 0:1], pick_at[:, 1:2]
    row_ids = iota((scens, local), 1) + share * local
    picks = (jnp.where(row_ids == pick_a, 1.0, 0.0) - jnp.where(row_ids == pick_b, 1.0, 0.0)).astype(bf16)
    tile = min(width, 512)
    depth_part = jnp.zeros((scens, 1), f32)
    for at in range(0, width, tile):
        piece = jnp.dot(picks, inverse_ref[:, at : at + tile], preferred_element_type=f32)
        branch_part[:, at : at + tile] = piece
        col_ids = iota((scens, tile), 1) + (half * width + at)
        signs = jnp.where(col_ids == pick_a, 1.0, 0.0) - jnp.where(col_ids == pick_b, 1.0, 0.0)
        depth_part = depth_part + jnp.sum(piece * signs, axis=1, keepdims=True)

    info_copy.wait()
    for copy in moved_buses:
        copy.wait()

    def gathered(ref):
        pieces = []
        for g in range(n // per_group):
            total = ref[g * per_group]
            for k in range(1, per_group):
                total = total + ref[g * per_group + k]
            pieces.append(total)
        return split_dot(jnp.concatenate(pieces, 1), order_ref[...])

    info = info_ref[...] + info_in[...]
    end_row = jnp.broadcast_to(info[past_rows + 2 : past_rows + 3], (16, ends))
    pts = jnp.concatenate([gathered(bus_in), end_row], 1)
    pts_col = pts.T[:, 0:1].astype(jnp.int32) - 1
    pts = pts[0:1].astype(jnp.int32) - 1
    own_pts = jnp.concatenate(
        [jnp.where(lower, pts[:, :cap], pts[:, cap : 2 * cap]), pts[:, 2 * cap :]], 1
    ) - half * width
    cols = cap + ends
    col_sel[...] = jnp.where(iota((width, cols), 0) == own_pts, 1.0, 0.0).astype(bf16)

    for at in range(0, local, 256):
        rows = slice(at, at + 256)
        narrow[rows, :] = jnp.dot(
            inverse_ref[rows, :], col_sel[...], preferred_element_type=f32
        ).astype(bf16)

    row_sel[...] = jnp.where(iota((points, local), 1) + share * local == pts_col, 1.0, 0.0).astype(bf16)
    part[...] = jnp.dot(row_sel[...], narrow[...], preferred_element_type=f32).astype(bf16)

    first = []
    for d in range(1, size):
        peer = (me + d) % size
        rows = pl.ds(pl.multiple_of(peer * block, 16), block)
        first.append(remote(part.at[rows], part_in.at[d - 1], group_sems.at[0, d], member(peer)))
    for copy in first:
        copy.start()
    side[:, :cols] = jnp.dot(picks, narrow[...], preferred_element_type=f32)
    side[:, cols:] = jnp.broadcast_to(depth_part, (scens, 128))
    sides = []
    for d in range(1, size):
        peer = (me + d) % size
        at = (share + groups - peer % groups + groups - 1) % groups
        rows = pl.ds(pl.multiple_of(at * scen, 8), scen)
        sides.append(remote(side.at[rows], side_in.at[d - 1], group_sems.at[1, d], member(peer)))
    for copy in sides:
        copy.start()
    volt_out[...] = split_dot(prev_ref[...], col_sel[:, :cap])
    volt_copy = remote(volt_out, volt_in, pair_sems.at[0], pair)
    volt_copy.start()
    for copy in moved_models:
        copy.start()
    model_in[place] = model_out[subnet]
    equal = pts == pts_col
    sub_at = iota((points, points), 0)
    leader = jnp.min(jnp.where(equal, sub_at.astype(f32), float(points)), axis=0, keepdims=True)
    leading = leader == iota((1, points), 1).astype(f32)
    merge[...] = jnp.where(equal & leading, 1.0, 0.0).astype(bf16)
    perm = jnp.where(
        iota((ends, ends), 0) == lanes_ref[0:1, :] + subnet * lanes_ref[2:3, :], 1.0, 0.0
    ).astype(bf16)
    own_rows = pl.ds(pl.multiple_of(me * block, 16), block)

    def placed(pieces):
        lows = jnp.zeros_like(pieces[0][1][:, :cap])
        highs = jnp.zeros_like(lows)
        rest = jnp.zeros_like(pieces[0][1][:, cap:])
        for from_lower, piece in pieces:
            lows = lows + jnp.where(from_lower, piece[:, :cap], 0.0)
            highs = highs + jnp.where(from_lower, 0.0, piece[:, :cap])
            rest = rest + piece[:, cap:]
        return lows, highs, rest

    pieces = [(lower, part[own_rows, :].astype(f32))]
    for d in range(1, size):
        first[d - 1].wait()
        pieces.append(((me + size - d) % size < groups, part_in[d - 1].astype(f32)))
    matrix[own_rows, :] = jnp.concatenate(placed(pieces), 1).astype(bf16)
    second = []
    for d in range(1, size):
        second.append(
            remote(matrix.at[own_rows], matrix.at[own_rows], group_sems.at[2, d], member((me + d) % size))
        )
    for copy in second:
        copy.start()

    pieces = [(lower, side[(groups - 1) * scen :, :])]
    for d in range(1, size):
        sides[d - 1].wait()
        pieces.append(((me + size - d) % size < groups, side_in[d - 1]))
    lows, highs, rest = placed(pieces)
    branch = jnp.concatenate([lows, highs, rest[:, :ends]], 1)
    depth = rest[:, ends : ends + 1]
    volt_copy.wait()
    own_volt, other_volt = volt_out[...], volt_in[...]
    volt = jnp.concatenate(
        [jnp.where(lower, own_volt, other_volt), jnp.where(lower, other_volt, own_volt)], 1
    )
    delays = info[past_rows : past_rows + 1]
    impedance = info[past_rows + 1 : past_rows + 2]
    admittance = 2.0 / jnp.where(delays == 0.0, 1.0, impedance)
    history = [info[k * 2 * scen : (k + 1) * 2 * scen] for k in range(depth_max)]
    for copy in moved_models:
        copy.wait()
    received = gathered(model_in)
    lag, gain = received[0:1], received[8:9]
    admit = switch_ref[:, 2:3]
    current = received[16 : 16 + scen]
    lines = []
    homes = []
    for step in range(steps):
        current = lag * current + gain * (received[16 + (step + 1) * scen : 16 + (step + 2) * scen] - volt)
        if step + 1 == steps:
            state_out[...] = jnp.where(lower, current[:, :cap], current[:, cap:])
            for d in range(1, n):
                homes.append(
                    remote(state_out, state_in.at[d - 1], home_sems.at[d], ((place + d) % n, share))
                )
            for copy in homes:
                copy.start()
        if step >= 2:
            for copy in lines[step - 2]:
                copy.wait()
            merged = jnp.zeros((2 * scen, ends), f32)
            for d in range(1, subs):
                moved = split_dot(line_in[step - 2, d - 1], perm)
                merged = merged + jnp.where(lanes_ref[1:2, :] == (subnet + subs - d) % subs, moved, 0.0)
            history.append(merged)
        line_term = jnp.zeros((scen, ends), f32)
        for delay in range(2, depth_max + 1):
            older = history[step - delay + depth_max]
            line_term = line_term + jnp.where(
                delays == delay, -admittance * older[:scen] - older[scen:], 0.0
            )
        feed = split_dot(jnp.concatenate([current, -line_term], 1), merge[...])
        rhs = feed.astype(bf16)
        along = jnp.sum(rhs.astype(f32) * branch, axis=1, keepdims=True)
        factor = admit * along / (1.0 + admit * depth)
        if step == 0:
            for copy in second:
                copy.wait()
        if step + 1 < steps:
            full = jnp.dot(rhs, matrix[...], preferred_element_type=f32) - factor * branch
            volt = full[:, : 2 * cap]
        if step + 2 < steps:
            line_out[step] = jnp.concatenate([full[:, 2 * cap :], line_term], 0)
            lines.append(
                [
                    remote(
                        line_out.at[step],
                        line_in.at[step, d - 1],
                        line_sems.at[step, d],
                        (((subnet + d) % subs) * 2 + half, share),
                    )
                    for d in range(1, subs)
                ]
            )
            for copy in lines[step]:
                copy.start()

    feed_out[...] = rhs
    factor_out[...] = jnp.broadcast_to(factor, factor_out.shape)
    shared = []
    for d in range(1, groups):
        device = (place, (share + d) % groups)
        shared.append(remote(feed_out, feed_in.at[d - 1], last_sems.at[0, d], device))
        shared.append(remote(factor_out, factor_in.at[d - 1], last_sems.at[1, d], device))
    for copy in shared:
        copy.start()
    for copy in shared:
        copy.wait()
    feeds = jnp.concatenate([feed_in[d - 1] for d in range(1, groups)] + [rhs], 0)
    dense = jnp.dot(feeds, row_sel[...], preferred_element_type=f32).astype(bf16)
    for at in range(0, width, tile):
        product = jnp.dot(dense, inverse_ref[:, at : at + tile], preferred_element_type=f32)
        for d in range(1, groups):
            rows = slice((d - 1) * scen, d * scen)
            partial_out[d - 1, :, at : at + tile] = (
                product[(d - 1) * scen : d * scen]
                - factor_in[d - 1][:, 0:1] * branch_part[rows, at : at + tile]
            )
        rows = slice((groups - 1) * scen, scens)
        voltage_ref[:, at : at + tile] = (
            product[(groups - 1) * scen :] - factor * branch_part[rows, at : at + tile]
        )
    partials = []
    for d in range(1, groups):
        device = (place, (share + groups - d) % groups)
        partials.append(remote(partial_out.at[d - 1], partial_in.at[d - 1], last_sems.at[2, d], device))
    for copy in partials:
        copy.start()
    for copy in homes:
        copy.wait()
    back = jnp.concatenate([state_out[...]] + [state_in[d - 1] for d in range(1, n)], 0)
    home = jnp.where(
        iota((cap, models), 0) == place * slots + rank_row.astype(jnp.int32), 1.0, 0.0
    ).astype(bf16)
    back = split_dot(back, home)
    out = jnp.zeros((scen, models), f32)
    for d in range(n):
        out = out + jnp.where(dest_row == (place + n - d) % n, back[d * scen : (d + 1) * scen], 0.0)
    current_ref[...] = out
    for copy in partials:
        copy.wait()
    total = voltage_ref[...]
    for d in range(1, groups):
        total = total + partial_in[d - 1]
    voltage_ref[...] = total


def per_device(
    inverse,
    voltage_prev,
    line_delay,
    line_bus,
    line_impedance,
    line_past,
    model_dest,
    model_bus,
    model_gain,
    model_lag,
    model_state,
    model_source,
    switch_bus,
    switch_admittance,
):
    n = lax.axis_size("rows")
    groups = lax.axis_size("scen")
    place = lax.axis_index("rows")
    share = lax.axis_index("scen")
    subnet = place // 2
    half = place % 2
    lower = half == 0
    depth_rows, width = inverse.shape
    scen = voltage_prev.shape[0]
    steps = model_source.shape[0]
    ends = line_bus.shape[1]
    models = model_bus.shape[0]
    depth_max = line_past.shape[0]
    slots = max(2, 2 * models // n)
    cap = n * slots
    f32, bf16 = jnp.float32, jnp.bfloat16

    pad = max(128, 2 * ends)
    points = 2 * cap + pad

    def end_lanes(values):
        none = jnp.zeros((values.shape[0], ends), values.dtype)
        both = jnp.where(
            lower, jnp.concatenate([values, none], 1), jnp.concatenate([none, values], 1)
        )
        return jnp.pad(both, ((0, 0), (0, pad - 2 * ends)))

    meta = jnp.stack([model_dest[:, 0].astype(f32), model_bus.astype(f32), model_lag, model_gain])
    meta = jnp.pad(meta, ((0, 4), (0, 0)))
    past = line_past[:, :, :, 0, :].reshape(depth_max * 2 * scen, ends)
    global_bus = (line_bus + half * width + 1).astype(f32)
    info = end_lanes(
        jnp.concatenate(
            [past, line_delay.astype(f32), line_impedance, global_bus, jnp.zeros((5, ends), f32)], 0
        )
    )
    switch_at = lax.dynamic_index_in_dim(switch_bus, subnet, axis=2, keepdims=False)
    admit = lax.dynamic_index_in_dim(switch_admittance, subnet, axis=1, keepdims=False)
    switch = jnp.stack([switch_at[0].astype(f32), switch_at[1].astype(f32), admit], 1)
    switch = jnp.pad(switch, ((0, 0), (0, 125)))

    lane = np.arange(2 * cap)
    comes = lane % cap // slots * 2 * slots + lane // cap * slots + lane % slots
    order = jnp.asarray(np.arange(2 * cap)[:, None] == comes[None, :], bf16)
    per_pair = ends // n
    lane = np.arange(pad)
    partner = lane % ends // per_pair
    origin = partner % 2 * ends + lane // ends * per_pair + lane % ends % per_pair
    live = lane < 2 * ends
    lanes = np.zeros((8, pad), np.int32)
    lanes[0] = np.where(live, origin, -1)
    lanes[1] = partner // 2
    lanes[2] = np.where(live, 2 * per_pair, 0)
    lanes = jnp.asarray(lanes)

    size = 2 * groups
    cols = cap + pad
    count = 16 + (steps + 1) * scen
    vmem = pl.BlockSpec(memory_space=pltpu.VMEM)
    voltage, model_current = pl.pallas_call(
        functools.partial(step_kernel, n, groups, steps, depth_max, cap, slots),
        out_shape=(
            jax.ShapeDtypeStruct((scen, width), f32),
            jax.ShapeDtypeStruct((scen, models), f32),
        ),
        in_specs=[vmem] * 9,
        out_specs=(vmem, vmem),
        scratch_shapes=[
            pltpu.VMEM((n // 2, 16, 128), f32),
            pltpu.VMEM((n, 16, 128), f32),
            pltpu.VMEM((groups - 1, scen, 128), f32),
            pltpu.VMEM((n // 2, count, 128), f32),
            pltpu.VMEM((n, count, 128), f32),
            pltpu.VMEM((width, cols), bf16),
            pltpu.VMEM((points, depth_rows), bf16),
            pltpu.VMEM((depth_rows, cols), bf16),
            pltpu.VMEM((points, points), bf16),
            pltpu.VMEM((groups * scen, width), f32),
            pltpu.VMEM((points, cols), bf16),
            pltpu.VMEM((groups * scen, cols + 128), f32),
            pltpu.VMEM((scen, cap), f32),
            pltpu.VMEM((size - 1, points // size, cols), bf16),
            pltpu.VMEM((size - 1, scen, cols + 128), f32),
            pltpu.VMEM((points, points), bf16),
            pltpu.VMEM((scen, cap), f32),
            pltpu.VMEM(info.shape, f32),
            pltpu.VMEM((steps - 2, 2 * scen, pad), f32),
            pltpu.VMEM((steps - 2, n // 2 - 1, 2 * scen, pad), f32),
            pltpu.VMEM((scen, points), bf16),
            pltpu.VMEM((groups - 1, scen, points), bf16),
            pltpu.VMEM((scen, 128), f32),
            pltpu.VMEM((groups - 1, scen, 128), f32),
            pltpu.VMEM((groups - 1, scen, width), f32),
            pltpu.VMEM((groups - 1, scen, width), f32),
            pltpu.VMEM((scen, cap), f32),
            pltpu.VMEM((n - 1, scen, cap), f32),
            pltpu.SemaphoreType.DMA((3, size, 2)),
            pltpu.SemaphoreType.DMA((2, 2)),
            pltpu.SemaphoreType.DMA((steps - 2, n // 2, 2)),
            pltpu.SemaphoreType.DMA((3, groups, 2)),
            pltpu.SemaphoreType.DMA((n, 2)),
            pltpu.SemaphoreType.DMA((n, 2)),
            pltpu.SemaphoreType.DMA((n, 2)),
            pltpu.SemaphoreType.DMA((groups, 2)),
        ],
        compiler_params=pltpu.CompilerParams(
            collective_id=0, has_side_effects=True, vmem_limit_bytes=56 * 2**20
        ),
    )(
        inverse,
        voltage_prev,
        meta,
        model_state,
        model_source.reshape(steps * scen, models),
        info,
        switch,
        order,
        lanes,
    )
    return (voltage, model_current)


def solution(mesh):
    placed = (
        P("scen", "rows"),
        P("scen", "rows"),
        P("rows", None),
        P("rows", None),
        P("rows", None),
        P(None, None, "scen", "rows", None),
        P("rows", None),
        P("rows"),
        P("rows"),
        P("rows"),
        P("scen", "rows"),
        P(None, "scen", "rows"),
        P(None, "scen", None),
        P("scen", None),
    )
    return jax.shard_map(
        per_device,
        mesh=mesh,
        in_specs=placed,
        out_specs=(P("scen", "rows"), P("scen", "rows")),
        check_vma=False,
    )
```
